32 devices in a mesh: feat: 2 (over x), store: 16 (over z, y, core).
Axes of the slice: x: 2, y: 2, z: 4, core: 2. Of those that a mesh axis runs over, the one named last changes fastest.
Arguments:
- layer_input: bfloat16 [8192, 8192], P('store', 'feat'), may hold values from -6 to 6
- out_grad: bfloat16 [8192, 8192], P('store', 'feat'), may hold values from -6 to 6
- proj_in: bfloat16 [8192, 256], P('feat'), may hold values from -0.0625 to 0.0625
- proj_out: bfloat16 [8192, 256], P('feat'), may hold values from -0.0625 to 0.0625
- inv_diag: float32 [65536], P('feat'), may hold values from 0.1 to 10
- stored: float32 [3072, 65536], P('store', 'feat'), may hold values from -0.0014648438 to 0.0014648438
- seq_lengths: int32 [16, 16], P('store'), may hold values from 1 to 64, 512 in all within a row
- query_order: int32 [16, 16], P('store'), may hold values from 0 to 15, as said below
Outputs:
- scores: float32 [256, 3072], P('feat', 'store')
The draws below stay inside these ranges and needn't reach their ends.
Inputs may be any that keep to these rules, and one draw needn't show every extreme that they name: `query_order`: each row is an ordering of the query slots 0 to 15, each slot once.
All inputs are finite; a program needn't handle non-finite values.
Results may differ from the reference program's by a relative error of at most 0.0003.
Values sent between devices are 32-bit elements; how exact they have to be, the bound alone decides.
No kernel may reach another device: no remote copies, remote signals or barrier semaphores. Data moves between devices by JAX's collectives and lax.ppermute only.
A program may use at most 128 MiB of HBM per device.

```python
import math
import jax
import jax.numpy as jnp
import numpy as np
from jax import lax

D = 8192
PIN = 256
POUT = 256
FEATS = 65536
TOK_DEV = 512
Q_DEV = 16
LMAX = 64
NBLK = 16
NTOK = 8192
NQ = 256
ROWS = 3072


def draw_query_order(key, part):
    keys = jax.random.split(jax.random.fold_in(key, 7), NBLK)
    orders = jax.vmap(lambda single: jax.random.permutation(single, Q_DEV))(keys)
    return orders.astype(jnp.int32)


def block_scale(stream_key, extent, cuts, least, top_value):
    def one(axis_at, shards_of):
        draws = jax.random.uniform(jax.random.fold_in(jax.random.fold_in(stream_key, 6), axis_at), (shards_of,), jnp.float32, least / len(cuts), top_value / len(cuts))
        return jnp.repeat(jnp.exp(draws), extent[axis_at] // shards_of).reshape((-1,) + (1,) * (len(extent) - axis_at - 1))

    factor_of = one(*cuts[0])
    for cut in cuts[1:]:
        factor_of = factor_of * one(*cut)
    return factor_of


def split_up(count, total, most, slope):
    weights = [(1 << 20) // math.isqrt(rank ** slope) + 1 for rank in range(2, count + 1)]
    rest, given = total - most - (count - 1), [1] * (count - 1)
    while rest > 0:
        free = [i for i in range(count - 1) if given[i] < most]
        whole, budget = sum([weights[i] for i in free]), rest
        for i in free:
            extra = min(most - given[i], max(1, budget * weights[i] // whole), rest)
            given[i] = given[i] + extra
            rest = rest - extra
    return np.array([most] + given)


def ragged_sizes(key, number_of, total, limit, lean):
    if number_of == 2:
        one = jax.random.randint(key, (), max(1, total - limit), min(limit, total - 1) + 1)
        return jnp.stack([one, total - one])
    tallies = jnp.asarray(split_up(number_of, total, limit, lean), jnp.int32)
    couples = (number_of - 1) // 2
    donor, sink = tallies[1:1 + 2 * couples:2], tallies[2:2 + 2 * couples:2]
    margin = jnp.minimum(donor - 1, limit - sink)
    shifted = jax.random.randint(jax.random.fold_in(key, 1), (couples,), 0, 1 << 20) % (margin + 1)
    tallies = tallies.at[1:1 + 2 * couples:2].set(donor - shifted).at[2:2 + 2 * couples:2].set(sink + shifted)
    return tallies[jax.random.permutation(jax.random.fold_in(key, 2), number_of)]


def normal_values(key, shape, deviation, most, shards=(), held_as=jnp.bfloat16):
    array = jax.random.normal(key, shape, jnp.float32) * deviation
    if len(shards) > 0:
        array = block_scale(key, shape, shards, -0.22, 0.18) * array
    return jnp.clip(array, min=-most, max=most).astype(held_as)


def setup_inputs(seed: int = 0) -> dict:
    streams_of = jax.random.split(jax.random.key(seed), 9)
    layer_input = normal_values(streams_of[0], (NTOK, D), 1.0, 6.0, ((0, 16), (1, 2)))
    out_grad = normal_values(streams_of[1], (NTOK, D), 1.0, 6.0, ((0, 16), (1, 2)))
    proj_in = normal_values(streams_of[2], (D, PIN), D ** -0.5, 0.0625, ((0, 2),))
    proj_out = normal_values(streams_of[3], (D, POUT), D ** -0.5, 0.0625, ((0, 2),))
    inv_diag = jnp.clip(jnp.exp(math.log(10.0) - 4.6051702 * jax.random.uniform(streams_of[4], (FEATS,), jnp.float32) ** block_scale(streams_of[4], (FEATS,), ((0, 2),), -0.2, 0.2)), 0.1, 10.0)
    stored = normal_values(streams_of[5], (ROWS, FEATS), (FEATS * 256) ** -0.5, 0.0014648438, ((0, 16), (1, 2)), jnp.float32)
    seq_lengths = jax.vmap(lambda own: ragged_sizes(own, Q_DEV, TOK_DEV, LMAX, 2))(jax.random.split(streams_of[6], NBLK)).reshape((NBLK, Q_DEV)).astype(jnp.int32)
    query_order = draw_query_order(jax.random.fold_in(streams_of[8], 71), 0)
    return dict(layer_input=layer_input, out_grad=out_grad, proj_in=proj_in, proj_out=proj_out, inv_diag=inv_diag, stored=stored, seq_lengths=seq_lengths, query_order=query_order)


def slot_matrix(lengths_row, order_row, count):
    ends = jnp.cumsum(lengths_row).astype(jnp.int32)
    position = jnp.arange(count, dtype=jnp.int32)
    segment = jnp.sum((position[:, None] >= ends[None, :]).astype(jnp.int32), axis=1)
    slots = jnp.arange(Q_DEV, dtype=jnp.int32)
    onehot = (segment[None, :] == slots[:, None]).astype(jnp.float32)
    mapping = (order_row[None, :] == slots[:, None]).astype(jnp.float32)
    return jnp.dot(mapping, onehot, precision=lax.Precision.HIGHEST)


def reference(layer_input, out_grad, proj_in, proj_out, inv_diag, stored, seq_lengths, query_order):
    inputs = layer_input.reshape(NBLK, TOK_DEV, D)
    grads = out_grad.reshape(NBLK, TOK_DEV, D)

    def one_block(packed):
        block_in, block_grad, lengths_row, order_row = packed
        in_proj = jnp.dot(block_in, proj_in, preferred_element_type=jnp.float32)
        grad_proj = jnp.dot(block_grad, proj_out, preferred_element_type=jnp.float32)
        member = slot_matrix(lengths_row, order_row, TOK_DEV)
        masked = member[:, :, None] * in_proj[None, :, :]
        query_grad = jnp.einsum("qti,tj->qij", masked, grad_proj, precision=lax.Precision.HIGHEST)
        query_grad = query_grad.reshape(Q_DEV, FEATS) * inv_diag[None, :]
        return jnp.einsum("qf,rf->qr", query_grad, stored, precision=lax.Precision.HIGHEST)

    result = lax.map(one_block, (inputs, grads, seq_lengths, query_order))
    return result.reshape(NQ, ROWS)
```

```python
import functools

import jax
import jax.numpy as jnp
from jax import lax
from jax.experimental import pallas as pl
from jax.experimental.pallas import tpu as pltpu
from jax.sharding import PartitionSpec as P


LANES = 128
MIB = 1024 * 1024


def chip_ring(devices):
    coords = [tuple(devices[0, s].coords) for s in range(0, devices.shape[1], 2)]
    count = len(coords)
    near = [
        [j for j in range(count) if sum(abs(a - b) for a, b in zip(coords[i], coords[j])) == 1]
        for i in range(count)
    ]

    def walk(path):
        if len(path) == count:
            return path if path[0] in near[path[-1]] else None
        for j in near[path[-1]]:
            if j not in path:
                found = walk(path + [j])
                if found:
                    return found
        return None

    return walk([0]) or list(range(count))


def split(x):
    high = x.astype(jnp.bfloat16)
    return high, (x - high.astype(jnp.float32)).astype(jnp.bfloat16)


def project_kernel(parts, extra, with_meta, feat_ref, x_ref, w_ref, *refs):
    if with_meta:
        len_ref, order_ref, *refs = refs
    keep_ref, *send_refs, acc_ref = refs
    k = pl.program_id(0)
    part = jnp.dot(x_ref[...], w_ref[...], preferred_element_type=jnp.float32)

    @pl.when(k == 0)
    def _():
        acc_ref[...] = part

    @pl.when(k > 0)
    def _():
        acc_ref[...] += part

    @pl.when(k == pl.num_programs(0) - 1)
    def _():
        rows, width = acc_ref.shape[0], acc_ref.shape[1] // parts
        pieces = [acc_ref[:, p * width : (p + 1) * width] for p in range(parts)]

        def piece(ahead):
            index = lax.rem(feat_ref[0] + ahead, parts)
            chosen = pieces[0]
            for p in range(1, parts):
                chosen = jnp.where(index == p, pieces[p], chosen)
            return chosen

        keep = piece(0)
        keep_ref[:rows, :] = keep
        for ahead, send_ref in enumerate(send_refs, 1):
            send = piece(ahead)
            send_ref[:rows, :] = send
            if extra:
                send_ref[rows:, :] = keep[:extra, :]
                keep_ref[rows:, :] = send[:extra, :]
            if with_meta:
                send_ref[rows:, :] = jnp.zeros((8, width), jnp.float32)
        if with_meta:
            slots = len_ref.shape[1]
            keep_ref[rows:, :] = jnp.zeros((8, width), jnp.float32)
            keep_ref[rows : rows + 1, :slots] = len_ref[...].astype(jnp.float32)
            keep_ref[rows + 1 : rows + 2, :slots] = order_ref[...].astype(jnp.float32)


def project(feat, parts, extra, x, w, meta=()):
    rows, depth = x.shape
    step = min(depth, 1024)
    width = w.shape[1] // parts
    tail = 8 if meta else extra
    out = jax.ShapeDtypeStruct((rows + tail, width), jnp.float32)
    whole = pl.BlockSpec((rows + tail, width), lambda k, f: (0, 0))
    return pl.pallas_call(
        functools.partial(project_kernel, parts, extra, bool(meta)),
        out_shape=(out,) * parts,
        grid_spec=pltpu.PrefetchScalarGridSpec(
            num_scalar_prefetch=1,
            grid=(depth // step,),
            in_specs=[
                pl.BlockSpec((rows, step), lambda k, f: (0, k)),
                pl.BlockSpec((step, w.shape[1]), lambda k, f: (k, 0)),
            ]
            + [pl.BlockSpec(m.shape, lambda k, f: (0, 0)) for m in meta],
            out_specs=(whole,) * parts,
            scratch_shapes=[pltpu.VMEM((rows, w.shape[1]), jnp.float32)],
        ),
        compiler_params=pltpu.CompilerParams(vmem_limit_bytes=16 * MIB),
    )(feat, x, w, *meta)


def score_kernel(blocks, slots, full, group, table_ref, *refs):
    a_refs, b_refs = refs[:blocks], refs[blocks : 2 * blocks]
    diag_ref, own_ref, other_ref, out_own_ref, out_other_ref = refs[2 * blocks : 2 * blocks + 5]
    meta_v, meta_s, grads, rows_buf, acc, acc_low, sem, meta_sem = refs[2 * blocks + 5 :]
    tokens = b_refs[0].shape[0]
    i_count, width = diag_ref.shape
    queries = blocks * slots
    rows = own_ref.shape[0]
    chunks = i_count // group
    ring = rows_buf.shape[0]
    offset = table_ref[blocks]

    def copies(chunk, slot):
        found = []
        for side, ref in enumerate((own_ref, other_ref)):
            into = rows_buf.at[slot, pl.ds(side * rows, rows)]
            if width == full:
                at = pl.multiple_of(chunk * group * full, LANES)
                found.append(pltpu.make_async_copy(ref.at[:, pl.ds(at, group * full)], into, sem.at[slot]))
            else:
                for g in range(group):
                    at = pl.multiple_of((chunk * group + g) * full + offset, LANES)
                    found.append(
                        pltpu.make_async_copy(
                            ref.at[:, pl.ds(at, width)], into.at[:, pl.ds(g * width, width)], sem.at[slot]
                        )
                    )
        return found

    for chunk in range(min(ring - 1, chunks)):
        for copy in copies(chunk, chunk):
            copy.start()

    for b, a_ref in enumerate(a_refs):
        meta_v[pl.ds(b * 8, 8), :] = a_ref[pl.ds(tokens, 8), :].astype(jnp.int32)
    meta_copy = pltpu.make_async_copy(meta_v, meta_s, meta_sem)
    meta_copy.start()
    meta_copy.wait()

    window = 80
    position = lax.broadcasted_iota(jnp.int32, (window, a_refs[0].shape[1]), 0)
    for b in range(blocks):
        a_ref, b_ref = a_refs[b], b_refs[b]
        base = table_ref[b] * slots

        def one(k, start, a_ref=a_ref, b_ref=b_ref, base=base, b=b):
            end = start + meta_s[b * 8, k]
            query = base + meta_s[b * 8 + 1, k]
            at = pl.multiple_of(jnp.minimum(start // 8 * 8, tokens - window), 8)
            token = position + at
            left = jnp.where((token >= start) & (token < end), a_ref[pl.ds(at, window), :], 0.0)
            left_high, left_low = split(left)
            right_high, right_low = split(b_ref[pl.ds(at, window), :])
            grad = lax.dot_general(
                jnp.concatenate([left_high, left_low, left_high], axis=0),
                jnp.concatenate([right_high, right_high, right_low], axis=0),
                (((0,), (0,)), ((), ())),
                preferred_element_type=jnp.float32,
            )
            grad = grad * diag_ref[...]
            for t in range(width // LANES):
                grads[t, pl.ds(query, i_count, stride=queries), :] = grad[:, t * LANES : (t + 1) * LANES]
            return end

        lax.fori_loop(0, slots, one, jnp.int32(0))

    acc[...] = jnp.zeros_like(acc)
    acc_low[...] = jnp.zeros_like(acc_low)
    contract = (((1,), (1,)), ((), ()))

    def chunk_step(chunk, carry):
        slot = lax.rem(chunk, ring)
        ahead = chunk + ring - 1

        @pl.when(ahead < chunks)
        def _():
            for copy in copies(ahead, lax.rem(ahead, ring)):
                copy.start()

        for copy in copies(chunk, slot):
            copy.wait()
        high, low = split(rows_buf[slot])
        grad = jnp.concatenate(
            [
                grads[t, pl.ds(pl.multiple_of((chunk * group + g) * queries, 8), queries), :]
                for g in range(group)
                for t in range(width // LANES)
            ],
            axis=1,
        )
        grad_high, grad_low = split(grad)
        both = jnp.concatenate([grad_high, grad_low], axis=0)
        acc[...] += lax.dot_general(high, both, contract, preferred_element_type=jnp.float32)
        acc_low[...] += lax.dot_general(low, grad_high, contract, preferred_element_type=jnp.float32)
        return carry

    lax.fori_loop(0, chunks, chunk_step, 0)
    total = acc[:, :queries] + acc[:, queries:] + acc_low[...]
    total = total.T
    out_own_ref[...] = total[:, :rows]
    out_other_ref[...] = total[:, rows:]


def score(table, a_pieces, b_pieces, diag, own, other, slots, full):
    blocks = len(a_pieces)
    queries = blocks * slots
    rows = own.shape[0]
    i_count, width = diag.shape
    group = max(1, 1024 // width)
    while i_count % group:
        group //= 2
    ring = 4
    vmem = pl.BlockSpec(memory_space=pltpu.VMEM)
    anywhere = pl.BlockSpec(memory_space=pl.ANY)
    out = jax.ShapeDtypeStruct((queries, rows), jnp.float32)
    return pl.pallas_call(
        functools.partial(score_kernel, blocks, slots, full, group),
        out_shape=(out, out),
        in_specs=[pl.BlockSpec(memory_space=pltpu.SMEM)] + [vmem] * (2 * blocks + 1) + [anywhere] * 2,
        out_specs=(vmem, vmem),
        scratch_shapes=[
            pltpu.VMEM((8 * blocks, i_count), jnp.int32),
            pltpu.SMEM((8 * blocks, i_count), jnp.int32),
            pltpu.VMEM((width // LANES, i_count * queries, LANES), jnp.float32),
            pltpu.VMEM((ring, 2 * rows, group * width), jnp.float32),
            pltpu.VMEM((2 * rows, 2 * queries), jnp.float32),
            pltpu.VMEM((2 * rows, queries), jnp.float32),
            pltpu.SemaphoreType.DMA((ring,)),
            pltpu.SemaphoreType.DMA,
        ],
        compiler_params=pltpu.CompilerParams(vmem_limit_bytes=36 * MIB),
    )(table, *a_pieces, *b_pieces, diag, own, other)


def solution(mesh):
    feats, stores = mesh.shape["feat"], mesh.shape["store"]
    ring = chip_ring(mesh.devices)
    chips = len(ring)
    place = {chip: at for at, chip in enumerate(ring)}
    axes = ("feat", "store")

    def links(shift=0, step=0, flip=0):
        pairs = []
        for f in range(feats):
            for s in range(stores):
                chip = ring[(place[s // 2] + step) % chips]
                pairs.append((f * stores + s, ((f + shift) % feats) * stores + 2 * chip + (s % 2 ^ flip)))
        return pairs

    def send(x, **where):
        return lax.ppermute(x, axes, links(**where))

    half = chips // 2
    steps = [0] + [d * r for r in range(1, half) for d in (1, -1)] + [half]
    origins = jnp.array([[ring[(place[c] - r) % chips] for r in steps] for c in range(chips)], jnp.int32)

    def body(layer_input, out_grad, proj_in, proj_out, inv_diag, stored, seq_lengths, query_order):
        feat = lax.axis_index("feat")
        store = lax.axis_index("store")
        core = lax.rem(store, 2)
        slots = query_order.shape[1]
        full = proj_out.shape[1]
        i_count = proj_in.shape[1] // feats
        j_part = full // feats
        rows = stored.shape[0]
        tokens = layer_input.shape[0]

        other_rows = send(stored, flip=1)
        feat_s = feat[None].astype(jnp.int32)
        b_keep, *b_send = project(feat_s, feats, 0, out_grad, proj_out)
        a_keep, *a_send = project(feat_s, feats, 0, layer_input, proj_in, (seq_lengths, query_order))
        b_own = b_keep
        for ahead, x in enumerate(b_send, 1):
            b_own = b_own + send(x, shift=ahead)
        a_own = a_keep
        for ahead, x in enumerate(a_send, 1):
            a_own = a_own + send(x, shift=ahead)

        a, b = {0: a_own}, {0: b_own}
        for r in range(1, half):
            for d in (1, -1):
                b[d * r] = send(b[d * (r - 1)], step=d)
                a[d * r] = send(a[d * (r - 1)], step=d)
        b[half] = send(b[half - 1], step=1)
        a[half] = send(a[1 - half], step=-1)
        cross = [
            {r: send(b[r], shift=ahead) for r in steps} for ahead in range(1, feats)
        ]

        origin = lax.dynamic_index_in_dim(origins, store // 2, 0, keepdims=False)
        diag = inv_diag.reshape(i_count, full)
        a_list = [a[r] for r in steps]
        if j_part % LANES == 0:
            results = []
            for ahead in range(feats):
                source = lax.rem(feat - ahead + feats, feats)
                pieces = [b[r] for r in steps] if ahead == 0 else [cross[ahead - 1][r] for r in steps]
                table = jnp.concatenate([origin, (source * j_part)[None].astype(jnp.int32)])
                part = lax.dynamic_slice_in_dim(diag, source * j_part, j_part, 1)
                results.append(score(table, a_list, pieces, part, stored, other_rows, slots, full))
            own, other = (sum(x[1:], x[0]) for x in zip(*results))
        else:
            pieces = []
            for r in steps:
                parts = [b[r]] + [cross[ahead - 1][r] for ahead in range(1, feats)]
                stacked = jnp.stack([parts[0]] + parts[:0:-1], axis=1)
                turned = jnp.roll(stacked, feat, axis=1)
                pieces.append(turned.reshape(tokens, full))
            table = jnp.concatenate([origin, jnp.zeros((1,), jnp.int32)])
            own, other = score(table, a_list, pieces, diag, stored, other_rows, slots, full)

        share = chips // feats * slots

        def portion(x, ahead):
            return lax.dynamic_slice_in_dim(x, lax.rem(feat + ahead, feats) * share, share, 0)

        near = portion(own, 0)
        far = send(portion(other, 0), flip=1)
        for ahead in range(1, feats):
            near = near + send(portion(own, ahead), shift=ahead)
            far = far + send(portion(other, ahead), shift=ahead, flip=1)
        near = near.reshape(-1, 1, slots, rows)
        far = far.reshape(-1, 1, slots, rows)
        first = jnp.where(core == 0, near, far)
        second = jnp.where(core == 0, far, near)
        return jnp.concatenate([first, second], axis=1).reshape(-1, rows)

    return jax.shard_map(
        body,
        mesh=mesh,
        in_specs=(
            P("store", "feat"),
            P("store", "feat"),
            P("feat", None),
            P("feat", None),
            P("feat"),
            P("store", "feat"),
            P("store", None),
            P("store", None),
        ),
        out_specs=P("feat", "store"),
        check_vma=False,
    )
```

```python
import functools

import jax
import jax.numpy as jnp
from jax import lax
from jax.experimental import pallas as pl
from jax.experimental.pallas import tpu as pltpu
from jax.sharding import PartitionSpec as P


LANES = 128
MIB = 1024 * 1024


def chip_ring(devices):
    coords = [tuple(devices[0, s].coords) for s in range(0, devices.shape[1], 2)]
    count = len(coords)
    near = [
        [j for j in range(count) if sum(abs(a - b) for a, b in zip(coords[i], coords[j])) == 1]
        for i in range(count)
    ]

    def walk(path):
        if len(path) == count:
            return path if path[0] in near[path[-1]] else None
        for j in near[path[-1]]:
            if j not in path:
                found = walk(path + [j])
                if found:
                    return found
        return None

    return walk([0]) or list(range(count))


def split(x):
    high = x.astype(jnp.bfloat16)
    return high, (x - high.astype(jnp.float32)).astype(jnp.bfloat16)


def project_kernel(parts, extra, with_meta, feat_ref, x_ref, w_ref, *refs):
    if with_meta:
        len_ref, order_ref, *refs = refs
    keep_ref, *send_refs, acc_ref = refs
    k = pl.program_id(0)
    part = jnp.dot(x_ref[...], w_ref[...], preferred_element_type=jnp.float32)

    @pl.when(k == 0)
    def _():
        acc_ref[...] = part

    @pl.when(k > 0)
    def _():
        acc_ref[...] += part

    @pl.when(k == pl.num_programs(0) - 1)
    def _():
        rows, width = acc_ref.shape[0], acc_ref.shape[1] // parts
        pieces = [acc_ref[:, p * width : (p + 1) * width] for p in range(parts)]

        def piece(ahead):
            index = lax.rem(feat_ref[0] + ahead, parts)
            chosen = pieces[0]
            for p in range(1, parts):
                chosen = jnp.where(index == p, pieces[p], chosen)
            return chosen

        keep = piece(0)
        keep_ref[:rows, :] = keep
        for ahead, send_ref in enumerate(send_refs, 1):
            send = piece(ahead)
            send_ref[:rows, :] = send
            if extra:
                send_ref[rows:, :] = keep[:extra, :]
                keep_ref[rows:, :] = send[:extra, :]
            if with_meta:
                send_ref[rows:, :] = jnp.zeros((8, width), jnp.float32)
        if with_meta:
            slots = len_ref.shape[1]
            keep_ref[rows:, :] = jnp.zeros((8, width), jnp.float32)
            keep_ref[rows : rows + 1, :slots] = len_ref[...].astype(jnp.float32)
            keep_ref[rows + 1 : rows + 2, :slots] = order_ref[...].astype(jnp.float32)


def project(feat, parts, extra, x, w, meta=()):
    rows, depth = x.shape
    step = min(depth, 1024)
    width = w.shape[1] // parts
    tail = 8 if meta else extra
    out = jax.ShapeDtypeStruct((rows + tail, width), jnp.float32)
    whole = pl.BlockSpec((rows + tail, width), lambda k, f: (0, 0))
    return pl.pallas_call(
        functools.partial(project_kernel, parts, extra, bool(meta)),
        out_shape=(out,) * parts,
        grid_spec=pltpu.PrefetchScalarGridSpec(
            num_scalar_prefetch=1,
            grid=(depth // step,),
            in_specs=[
                pl.BlockSpec((rows, step), lambda k, f: (0, k)),
                pl.BlockSpec((step, w.shape[1]), lambda k, f: (k, 0)),
            ]
            + [pl.BlockSpec(m.shape, lambda k, f: (0, 0)) for m in meta],
            out_specs=(whole,) * parts,
            scratch_shapes=[pltpu.VMEM((rows, w.shape[1]), jnp.float32)],
        ),
        compiler_params=pltpu.CompilerParams(vmem_limit_bytes=16 * MIB),
    )(feat, x, w, *meta)


def score_kernel(blocks, slots, full, group, table_ref, *refs):
    a_refs, b_refs = refs[:blocks], refs[blocks : 2 * blocks]
    diag_ref, own_ref, other_ref, out_own_ref, out_other_ref = refs[2 * blocks : 2 * blocks + 5]
    meta_v, meta_s, grads, rows_buf, acc, acc_low, sem, meta_sem = refs[2 * blocks + 5 :]
    tokens = b_refs[0].shape[0]
    i_count, width = diag_ref.shape
    queries = blocks * slots
    rows = own_ref.shape[0]
    chunks = i_count // group
    ring = rows_buf.shape[0]
    offset = table_ref[blocks]

    def copies(chunk, slot):
        found = []
        for side, ref in enumerate((own_ref, other_ref)):
            into = rows_buf.at[slot, pl.ds(side * rows, rows)]
            if width == full:
                at = pl.multiple_of(chunk * group * full, LANES)
                found.append(pltpu.make_async_copy(ref.at[:, pl.ds(at, group * full)], into, sem.at[slot]))
            else:
                for g in range(group):
                    at = pl.multiple_of((chunk * group + g) * full + offset, LANES)
                    found.append(
                        pltpu.make_async_copy(
                            ref.at[:, pl.ds(at, width)], into.at[:, pl.ds(g * width, width)], sem.at[slot]
                        )
                    )
        return found

    for chunk in range(min(ring - 1, chunks)):
        for copy in copies(chunk, chunk):
            copy.start()

    for b, a_ref in enumerate(a_refs):
        meta_v[pl.ds(b * 8, 8), :] = a_ref[pl.ds(tokens, 8), :].astype(jnp.int32)
    meta_copy = pltpu.make_async_copy(meta_v, meta_s, meta_sem)
    meta_copy.start()
    meta_copy.wait()

    window = 80
    position = lax.broadcasted_iota(jnp.int32, (window, a_refs[0].shape[1]), 0)
    for b in range(blocks):
        a_ref, b_ref = a_refs[b], b_refs[b]
        base = table_ref[b] * slots

        def one(k, start, a_ref=a_ref, b_ref=b_ref, base=base, b=b):
            end = start + meta_s[b * 8, k]
            query = base + meta_s[b * 8 + 1, k]
            at = pl.multiple_of(jnp.minimum(start // 8 * 8, tokens - window), 8)
            token = position + at
            left = jnp.where((token >= start) & (token < end), a_ref[pl.ds(at, window), :], 0.0)
            left_high, left_low = split(left)
            right_high, right_low = split(b_ref[pl.ds(at, window), :])
            grad = lax.dot_general(
                jnp.concatenate([left_high, left_low, left_high], axis=0),
                jnp.concatenate([right_high, right_high, right_low], axis=0),
                (((0,), (0,)), ((), ())),
                preferred_element_type=jnp.float32,
            )
            grad = grad * diag_ref[...]
            for t in range(width // LANES):
                grads[t, pl.ds(query, i_count, stride=queries), :] = grad[:, t * LANES : (t + 1) * LANES]
            return end

        lax.fori_loop(0, slots, one, jnp.int32(0), unroll=4)

    acc[...] = jnp.zeros_like(acc)
    acc_low[...] = jnp.zeros_like(acc_low)
    contract = (((1,), (1,)), ((), ()))

    def chunk_step(chunk, carry):
        slot = lax.rem(chunk, ring)
        ahead = chunk + ring - 1

        @pl.when(ahead < chunks)
        def _():
            for copy in copies(ahead, lax.rem(ahead, ring)):
                copy.start()

        for copy in copies(chunk, slot):
            copy.wait()
        high, low = split(rows_buf[slot])
        grad = jnp.concatenate(
            [
                grads[t, pl.ds(pl.multiple_of((chunk * group + g) * queries, 8), queries), :]
                for g in range(group)
                for t in range(width // LANES)
            ],
            axis=1,
        )
        grad_high, grad_low = split(grad)
        both = jnp.concatenate([grad_high, grad_low], axis=0)
        acc[...] += lax.dot_general(high, both, contract, preferred_element_type=jnp.float32)
        acc_low[...] += lax.dot_general(low, grad_high, contract, preferred_element_type=jnp.float32)
        return carry

    lax.fori_loop(0, chunks, chunk_step, 0)
    total = acc[:, :queries] + acc[:, queries:] + acc_low[...]
    total = total.T
    out_own_ref[...] = total[:, :rows]
    out_other_ref[...] = total[:, rows:]


def score(table, a_pieces, b_pieces, diag, own, other, slots, full):
    blocks = len(a_pieces)
    queries = blocks * slots
    rows = own.shape[0]
    i_count, width = diag.shape
    group = max(1, 1024 // width)
    while i_count % group:
        group //= 2
    ring = 4
    vmem = pl.BlockSpec(memory_space=pltpu.VMEM)
    anywhere = pl.BlockSpec(memory_space=pl.ANY)
    out = jax.ShapeDtypeStruct((queries, rows), jnp.float32)
    return pl.pallas_call(
        functools.partial(score_kernel, blocks, slots, full, group),
        out_shape=(out, out),
        in_specs=[pl.BlockSpec(memory_space=pltpu.SMEM)] + [vmem] * (2 * blocks + 1) + [anywhere] * 2,
        out_specs=(vmem, vmem),
        scratch_shapes=[
            pltpu.VMEM((8 * blocks, i_count), jnp.int32),
            pltpu.SMEM((8 * blocks, i_count), jnp.int32),
            pltpu.VMEM((width // LANES, i_count * queries, LANES), jnp.float32),
            pltpu.VMEM((ring, 2 * rows, group * width), jnp.float32),
            pltpu.VMEM((2 * rows, 2 * queries), jnp.float32),
            pltpu.VMEM((2 * rows, queries), jnp.float32),
            pltpu.SemaphoreType.DMA((ring,)),
            pltpu.SemaphoreType.DMA,
        ],
        compiler_params=pltpu.CompilerParams(vmem_limit_bytes=36 * MIB),
    )(table, *a_pieces, *b_pieces, diag, own, other)


def solution(mesh):
    feats, stores = mesh.shape["feat"], mesh.shape["store"]
    ring = chip_ring(mesh.devices)
    chips = len(ring)
    place = {chip: at for at, chip in enumerate(ring)}
    axes = ("feat", "store")

    def links(shift=0, step=0, flip=0):
        pairs = []
        for f in range(feats):
            for s in range(stores):
                chip = ring[(place[s // 2] + step) % chips]
                pairs.append((f * stores + s, ((f + shift) % feats) * stores + 2 * chip + (s % 2 ^ flip)))
        return pairs

    def send(x, **where):
        return lax.ppermute(x, axes, links(**where))

    half = chips // 2
    steps = [0] + [d * r for r in range(1, half) for d in (1, -1)] + [half]
    origins = jnp.array([[ring[(place[c] - r) % chips] for r in steps] for c in range(chips)], jnp.int32)

    def body(layer_input, out_grad, proj_in, proj_out, inv_diag, stored, seq_lengths, query_order):
        feat = lax.axis_index("feat")
        store = lax.axis_index("store")
        core = lax.rem(store, 2)
        slots = query_order.shape[1]
        full = proj_out.shape[1]
        i_count = proj_in.shape[1] // feats
        j_part = full // feats
        rows = stored.shape[0]
        tokens = layer_input.shape[0]

        other_rows = send(stored, flip=1)
        feat_s = feat[None].astype(jnp.int32)
        b_keep, *b_send = project(feat_s, feats, 0, out_grad, proj_out)
        a_keep, *a_send = project(feat_s, feats, 0, layer_input, proj_in, (seq_lengths, query_order))
        b_own = b_keep
        for ahead, x in enumerate(b_send, 1):
            b_own = b_own + send(x, shift=ahead)
        a_own = a_keep
        for ahead, x in enumerate(a_send, 1):
            a_own = a_own + send(x, shift=ahead)

        a, b = {0: a_own}, {0: b_own}
        for r in range(1, half):
            for d in (1, -1):
                b[d * r] = send(b[d * (r - 1)], step=d)
                a[d * r] = send(a[d * (r - 1)], step=d)
        b[half] = send(b[half - 1], step=1)
        a[half] = send(a[1 - half], step=-1)
        cross = [
            {r: send(b[r], shift=ahead) for r in steps} for ahead in range(1, feats)
        ]

        origin = lax.dynamic_index_in_dim(origins, store // 2, 0, keepdims=False)
        diag = inv_diag.reshape(i_count, full)
        a_list = [a[r] for r in steps]
        if j_part % LANES == 0:
            results = []
            for ahead in range(feats):
                source = lax.rem(feat - ahead + feats, feats)
                pieces = [b[r] for r in steps] if ahead == 0 else [cross[ahead - 1][r] for r in steps]
                table = jnp.concatenate([origin, (source * j_part)[None].astype(jnp.int32)])
                part = lax.dynamic_slice_in_dim(diag, source * j_part, j_part, 1)
                results.append(score(table, a_list, pieces, part, stored, other_rows, slots, full))
            own, other = (sum(x[1:], x[0]) for x in zip(*results))
        else:
            pieces = []
            for r in steps:
                parts = [b[r]] + [cross[ahead - 1][r] for ahead in range(1, feats)]
                stacked = jnp.stack([parts[0]] + parts[:0:-1], axis=1)
                turned = jnp.roll(stacked, feat, axis=1)
                pieces.append(turned.reshape(tokens, full))
            table = jnp.concatenate([origin, jnp.zeros((1,), jnp.int32)])
            own, other = score(table, a_list, pieces, diag, stored, other_rows, slots, full)

        share = chips // feats * slots

        def portion(x, ahead):
            return lax.dynamic_slice_in_dim(x, lax.rem(feat + ahead, feats) * share, share, 0)

        near = portion(own, 0)
        far = send(portion(other, 0), flip=1)
        for ahead in range(1, feats):
            near = near + send(portion(own, ahead), shift=ahead)
            far = far + send(portion(other, ahead), shift=ahead, flip=1)
        near = near.reshape(-1, 1, slots, rows)
        far = far.reshape(-1, 1, slots, rows)
        first = jnp.where(core == 0, near, far)
        second = jnp.where(core == 0, far, near)
        return jnp.concatenate([first, second], axis=1).reshape(-1, rows)

    return jax.shard_map(
        body,
        mesh=mesh,
        in_specs=(
            P("store", "feat"),
            P("store", "feat"),
            P("feat", None),
            P("feat", None),
            P("feat"),
            P("store", "feat"),
            P("store", None),
            P("store", None),
        ),
        out_specs=P("feat", "store"),
        check_vma=False,
    )
```

```python
import functools

import jax
import jax.numpy as jnp
from jax import lax
from jax.experimental import pallas as pl
from jax.experimental.pallas import tpu as pltpu
from jax.sharding import PartitionSpec as P


LANES = 128
MIB = 1024 * 1024
WINDOW = 80


def chip_ring(devices):
    coords = [tuple(devices[0, s].coords) for s in range(0, devices.shape[1], 2)]
    count = len(coords)
    near = [
        [j for j in range(count) if sum(abs(a - b) for a, b in zip(coords[i], coords[j])) == 1]
        for i in range(count)
    ]

    def walk(path):
        if len(path) == count:
            return path if path[0] in near[path[-1]] else None
        for j in near[path[-1]]:
            if j not in path:
                found = walk(path + [j])
                if found:
                    return found
        return None

    return walk([0]) or list(range(count))


def in_hbm(x):
    return pltpu.with_memory_space_constraint(x, pltpu.HBM)


def split(x):
    high = x.astype(jnp.bfloat16)
    return high, (x - high.astype(jnp.float32)).astype(jnp.bfloat16)


def project_kernel(parts, extra, feat_ref, x_hbm, w_hbm, *refs):
    meta_refs, refs = refs[: -(parts + 3)], refs[-(parts + 3) :]
    keep_ref, *send_refs = refs[:parts]
    x_buf, w_buf, sem = refs[parts:]
    steps, rows, step = x_buf.shape
    copies = []
    for k in range(steps):
        at = pl.ds(k * step, step)
        pair = (
            pltpu.make_async_copy(x_hbm.at[:, at], x_buf.at[k], sem.at[k]),
            pltpu.make_async_copy(w_hbm.at[at, :], w_buf.at[at, :], sem.at[k]),
        )
        for copy in pair:
            copy.start()
        copies.append(pair)
    total = None
    for k in range(steps):
        for copy in copies[k]:
            copy.wait()
        part = jnp.dot(x_buf[k], w_buf[pl.ds(k * step, step), :], preferred_element_type=jnp.float32)
        total = part if total is None else total + part

    width = total.shape[1] // parts
    pieces = [total[:, p * width : (p + 1) * width] for p in range(parts)]

    def piece(ahead):
        index = lax.rem(feat_ref[0] + ahead, parts)
        chosen = pieces[0]
        for p in range(1, parts):
            chosen = jnp.where(index == p, pieces[p], chosen)
        return chosen

    keep = piece(0)
    keep_ref[:rows, :] = keep
    for ahead, send_ref in enumerate(send_refs, 1):
        send = piece(ahead)
        send_ref[:rows, :] = send
        if extra:
            send_ref[rows:, :] = keep[:extra, :]
            keep_ref[rows:, :] = send[:extra, :]
        if meta_refs:
            send_ref[rows:, :] = jnp.zeros((8, width), jnp.float32)
    if meta_refs:
        keep_ref[rows:, :] = jnp.zeros((8, width), jnp.float32)
        for row, ref in enumerate(meta_refs):
            keep_ref[rows + row : rows + row + 1, : ref.shape[1]] = ref[...].astype(jnp.float32)


def project(feat, parts, extra, x, w, meta=()):
    rows, depth = x.shape
    step = min(depth, 1024)
    steps = depth // step
    tail = 8 if meta else extra
    vmem = pl.BlockSpec(memory_space=pltpu.VMEM)
    hbm = pl.BlockSpec(memory_space=pltpu.HBM)
    out = jax.ShapeDtypeStruct((rows + tail, w.shape[1] // parts), jnp.float32)
    return pl.pallas_call(
        functools.partial(project_kernel, parts, extra),
        out_shape=(out,) * parts,
        in_specs=[pl.BlockSpec(memory_space=pltpu.SMEM), hbm, hbm] + [vmem] * len(meta),
        out_specs=(vmem,) * parts,
        scratch_shapes=[
            pltpu.VMEM((steps, rows, step), x.dtype),
            pltpu.VMEM(w.shape, w.dtype),
            pltpu.SemaphoreType.DMA((steps,)),
        ],
        compiler_params=pltpu.CompilerParams(vmem_limit_bytes=14 * MIB),
    )(feat, x, w, *meta)


def form_kernel(blocks, slots, *refs):
    a_refs, b_refs = refs[:blocks], refs[blocks : 2 * blocks]
    diag_ref, out_ref, meta_v, meta_s, grads, meta_sem, out_sem = refs[2 * blocks :]
    tokens = b_refs[0].shape[0]
    i_count, width = diag_ref.shape
    pitch = grads.shape[2]
    flat = grads.reshape(width // LANES, i_count * pitch, LANES)

    for b, a_ref in enumerate(a_refs):
        meta_v[pl.ds(b * 8, 8), :] = a_ref[pl.ds(tokens, 8), :].astype(jnp.int32)
    meta_copy = pltpu.make_async_copy(meta_v, meta_s, meta_sem)
    meta_copy.start()
    meta_copy.wait()

    position = lax.broadcasted_iota(jnp.int32, (WINDOW, a_refs[0].shape[1]), 0)
    outs = []
    for b in range(blocks):
        a_ref, b_ref = a_refs[b], b_refs[b]

        def one(k, start, a_ref=a_ref, b_ref=b_ref, b=b):
            end = start + meta_s[b * 8, k]
            query = b * slots + meta_s[b * 8 + 1, k]
            at = pl.multiple_of(jnp.minimum(start // 8 * 8, tokens - WINDOW), 8)
            token = position + at
            left = jnp.where((token >= start) & (token < end), a_ref[pl.ds(at, WINDOW), :], 0.0)
            left_high, left_low = split(left)
            right_high, right_low = split(b_ref[pl.ds(at, WINDOW), :])
            grad = lax.dot_general(
                jnp.concatenate([left_high, left_low, left_high], axis=0),
                jnp.concatenate([right_high, right_high, right_low], axis=0),
                (((0,), (0,)), ((), ())),
                preferred_element_type=jnp.float32,
            )
            grad = grad * diag_ref[...]
            for t in range(width // LANES):
                flat[t, pl.ds(query, i_count, stride=pitch), :] = grad[:, t * LANES : (t + 1) * LANES]
            return end

        lax.fori_loop(0, slots, one, jnp.int32(0), unroll=4)
        at = pl.ds(b * slots, slots)
        out = pltpu.make_async_copy(grads.at[:, :, at, :], out_ref.at[:, :, at, :], out_sem.at[b])
        out.start()
        outs.append(out)
    for out in outs:
        out.wait()


def form(a_pieces, b_pieces, diag, slots):
    blocks = len(a_pieces)
    i_count, width = diag.shape
    queries = blocks * slots
    pitch = queries + 8 if queries % 16 == 0 else queries
    vmem = pl.BlockSpec(memory_space=pltpu.VMEM)
    return pl.pallas_call(
        functools.partial(form_kernel, blocks, slots),
        out_shape=jax.ShapeDtypeStruct((width // LANES, i_count, queries, LANES), jnp.float32),
        in_specs=[vmem] * (2 * blocks + 1),
        out_specs=pl.BlockSpec(memory_space=pl.ANY),
        scratch_shapes=[
            pltpu.VMEM((8 * blocks, i_count), jnp.int32),
            pltpu.SMEM((8 * blocks, i_count), jnp.int32),
            pltpu.VMEM((width // LANES, i_count, pitch, LANES), jnp.float32),
            pltpu.SemaphoreType.DMA,
            pltpu.SemaphoreType.DMA((blocks,)),
        ],
        compiler_params=pltpu.CompilerParams(vmem_limit_bytes=12 * MIB),
    )(*a_pieces, *b_pieces, diag)


def score_kernel(counts, slots, full, group, table_ref, *refs):
    parts = len(counts)
    grad_refs = refs[:parts]
    own_ref, other_ref, out_own_ref, out_other_ref, rows_buf, grad_buf, acc, acc_low, sem = refs[parts:]
    blocks = sum(counts)
    tiles, i_count = grad_refs[0].shape[:2]
    width = tiles * LANES
    queries = blocks * slots
    rows = own_ref.shape[0]
    chunks = i_count // group
    ring = rows_buf.shape[0]
    offset = table_ref[blocks]

    def lanes(chunk, g):
        if width == full:
            return pl.ds(pl.multiple_of(chunk * group * full, LANES), group * full)
        return pl.ds(pl.multiple_of((chunk * group + g) * full + offset, LANES), width)

    spans = 1 if width == full else group

    def copies(chunk, slot):
        found = []
        for g in range(spans):
            size = group * width // spans
            for side, ref in enumerate((own_ref, other_ref)):
                into = rows_buf.at[slot, pl.ds(side * rows, rows), pl.ds(g * size, size)]
                found.append(pltpu.make_async_copy(ref.at[:, lanes(chunk, g)], into, sem.at[slot]))
        at = 0
        for count, ref in zip(counts, grad_refs):
            size = count * slots
            found.append(
                pltpu.make_async_copy(
                    ref.at[:, pl.ds(chunk * group, group)], grad_buf.at[slot, :, :, pl.ds(at, size)], sem.at[slot]
                )
            )
            at += size
        return found

    for chunk in range(min(ring - 1, chunks)):
        for copy in copies(chunk, chunk):
            copy.start()

    acc[...] = jnp.zeros_like(acc)
    acc_low[...] = jnp.zeros_like(acc_low)
    contract = (((1,), (1,)), ((), ()))

    def chunk_step(chunk, carry):
        slot = lax.rem(chunk, ring)
        ahead = chunk + ring - 1

        @pl.when(ahead < chunks)
        def _():
            for copy in copies(ahead, lax.rem(ahead, ring)):
                copy.start()

        for copy in copies(chunk, slot):
            copy.wait()
        high, low = split(rows_buf[slot])
        grad = jnp.concatenate([grad_buf[slot, t, g] for g in range(group) for t in range(tiles)], axis=1)
        grad_high, grad_low = split(grad)
        both = jnp.concatenate([grad_high, grad_low], axis=0)
        acc[...] += lax.dot_general(high, both, contract, preferred_element_type=jnp.float32)
        acc_low[...] += lax.dot_general(low, grad_high, contract, preferred_element_type=jnp.float32)
        return carry

    lax.fori_loop(0, chunks, chunk_step, 0)
    total = acc[:, :queries] + acc[:, queries:] + acc_low[...]
    total = total.T
    for b in range(blocks):
        at = pl.ds(pl.multiple_of(table_ref[b] * slots, slots), slots)
        piece = total[b * slots : (b + 1) * slots, :]
        out_own_ref[at, :] = piece[:, :rows]
        out_other_ref[at, :] = piece[:, rows:]


def score(table, grads, own, other, slots, full):
    counts = [x.shape[2] // slots for x in grads]
    queries = sum(counts) * slots
    rows = own.shape[0]
    tiles, i_count = grads[0].shape[:2]
    width = tiles * LANES
    group = max(1, 1024 // width)
    while i_count % group:
        group //= 2
    ring = 4
    vmem = pl.BlockSpec(memory_space=pltpu.VMEM)
    anywhere = pl.BlockSpec(memory_space=pl.ANY)
    out = jax.ShapeDtypeStruct((queries, rows), jnp.float32)
    return pl.pallas_call(
        functools.partial(score_kernel, counts, slots, full, group),
        out_shape=(out, out),
        in_specs=[pl.BlockSpec(memory_space=pltpu.SMEM)] + [anywhere] * (len(grads) + 2),
        out_specs=(vmem, vmem),
        scratch_shapes=[
            pltpu.VMEM((ring, 2 * rows, group * width), jnp.float32),
            pltpu.VMEM((ring, tiles, group, queries, LANES), jnp.float32),
            pltpu.VMEM((2 * rows, 2 * queries), jnp.float32),
            pltpu.VMEM((2 * rows, queries), jnp.float32),
            pltpu.SemaphoreType.DMA((ring,)),
        ],
        compiler_params=pltpu.CompilerParams(vmem_limit_bytes=16 * MIB),
    )(table, *grads, own, other)


def solution(mesh):
    feats, stores = mesh.shape["feat"], mesh.shape["store"]
    ring = chip_ring(mesh.devices)
    chips = len(ring)
    place = {chip: at for at, chip in enumerate(ring)}
    axes = ("feat", "store")

    def links(shift=0, step=0, flip=0):
        pairs = []
        for f in range(feats):
            for s in range(stores):
                chip = ring[(place[s // 2] + step) % chips]
                pairs.append((f * stores + s, ((f + shift) % feats) * stores + 2 * chip + (s % 2 ^ flip)))
        return pairs

    def send(x, **where):
        return lax.ppermute(x, axes, links(**where))

    half = chips // 2
    steps = [0] + [d * r for r in range(1, half) for d in (1, -1)] + [half]
    origins = jnp.array([[ring[(place[c] - r) % chips] for r in steps] for c in range(chips)], jnp.int32)

    def body(layer_input, out_grad, proj_in, proj_out, inv_diag, stored, seq_lengths, query_order):
        feat = lax.axis_index("feat")
        store = lax.axis_index("store")
        core = lax.rem(store, 2)
        slots = query_order.shape[1]
        full = proj_out.shape[1]
        i_count = proj_in.shape[1] // feats
        j_part = full // feats
        rows = stored.shape[0]
        tokens = layer_input.shape[0]

        other_rows = in_hbm(send(stored, flip=1))
        layer_input, out_grad, proj_in, proj_out, stored = map(
            in_hbm, (layer_input, out_grad, proj_in, proj_out, stored)
        )
        feat_s = feat[None].astype(jnp.int32)
        b_keep, *b_send = project(feat_s, feats, 0, out_grad, proj_out)
        a_keep, *a_send = project(feat_s, feats, 0, layer_input, proj_in, (seq_lengths, query_order))
        b_own = b_keep
        for ahead, x in enumerate(b_send, 1):
            b_own = b_own + send(x, shift=ahead)
        a_own = a_keep
        for ahead, x in enumerate(a_send, 1):
            a_own = a_own + send(x, shift=ahead)

        a, b = {0: a_own}, {0: b_own}
        for r in range(1, half):
            for d in (1, -1):
                b[d * r] = send(b[d * (r - 1)], step=d)
                a[d * r] = send(a[d * (r - 1)], step=d)
        b[half] = send(b[half - 1], step=1)
        a[half] = send(a[1 - half], step=-1)
        cross = [
            {r: send(b[r], shift=ahead) for r in steps} for ahead in range(1, feats)
        ]

        origin = lax.dynamic_index_in_dim(origins, store // 2, 0, keepdims=False)
        diag = inv_diag.reshape(i_count, full)
        rounds = [steps[:3]] + [steps[at : at + 2] for at in range(3, len(steps), 2)]
        if j_part % LANES == 0:
            results = []
            for ahead in range(feats):
                source = lax.rem(feat - ahead + feats, feats)
                pieces = b if ahead == 0 else cross[ahead - 1]
                table = jnp.concatenate([origin, (source * j_part)[None].astype(jnp.int32)])
                part = lax.dynamic_slice_in_dim(diag, source * j_part, j_part, 1)
                grads = [form([a[r] for r in g], [pieces[r] for r in g], part, slots) for g in rounds]
                results.append(score(table, grads, stored, other_rows, slots, full))
            own, other = (sum(x[1:], x[0]) for x in zip(*results))
        else:
            pieces = {}
            for r in steps:
                parts = [b[r]] + [cross[ahead - 1][r] for ahead in range(1, feats)]
                stacked = jnp.stack([parts[0]] + parts[:0:-1], axis=1)
                turned = jnp.roll(stacked, feat, axis=1)
                pieces[r] = turned.reshape(tokens, full)
            table = jnp.concatenate([origin, jnp.zeros((1,), jnp.int32)])
            grads = [form([a[r] for r in g], [pieces[r] for r in g], diag, slots) for g in rounds]
            own, other = score(table, grads, stored, other_rows, slots, full)

        share = chips // feats * slots

        def portion(x, ahead):
            return lax.dynamic_slice_in_dim(x, lax.rem(feat + ahead, feats) * share, share, 0)

        near = portion(own, 0)
        far = send(portion(other, 0), flip=1)
        for ahead in range(1, feats):
            near = near + send(portion(own, ahead), shift=ahead)
            far = far + send(portion(other, ahead), shift=ahead, flip=1)
        near = near.reshape(-1, 1, slots, rows)
        far = far.reshape(-1, 1, slots, rows)
        first = jnp.where(core == 0, near, far)
        second = jnp.where(core == 0, far, near)
        return jnp.concatenate([first, second], axis=1).reshape(-1, rows)

    return jax.shard_map(
        body,
        mesh=mesh,
        in_specs=(
            P("store", "feat"),
            P("store", "feat"),
            P("feat", None),
            P("feat", None),
            P("feat"),
            P("store", "feat"),
            P("store", None),
            P("store", None),
        ),
        out_specs=P("feat", "store"),
        check_vma=False,
    )
```
